32 devices in a mesh: gx: 8 (over z, core), gy: 4 (over y, x).
Axes of the slice: x: 2, y: 2, z: 4, core: 2. Of those that a mesh axis runs over, the one named last changes fastest.
Arguments:
- dtn_maps: float32 [8, 4, 1024, 1024], P('gx', 'gy'), may hold values from -8 to 25, as said below
- flux_part: float32 [8, 4, 1024, 32], P('gx', 'gy'), may hold values from -6 to 6
- outer_values: float32 [8, 4, 512, 32], P('gx', 'gy'), may hold values from -6 to 6
Outputs:
- merged_map: float32 [8, 4, 512, 2048], P('gx', 'gy')
- merged_flux: float32 [8, 4, 512, 32], P('gx', 'gy')
- box_values: float32 [8, 4, 1024, 32], P('gx', 'gy')
The draws below stay inside these ranges and needn't reach their ends.
Inputs may be any that keep to these rules, and one draw needn't show every extreme that they name: `dtn_maps`: each box's map is symmetric positive definite.
All inputs are finite; a program needn't handle non-finite values.
Results may differ from the reference program's by a relative error of at most 0.00005.
Values sent between devices are 32-bit elements; how exact they have to be, the bound alone decides.
A program may use at most 128 MiB of HBM per device.

```python
import jax
import jax.numpy as jnp
from jax import lax

EDGE = 256
RHS = 32
BOUND = 1024
NBX = 8
NBY = 4


def draw_dtn_maps(key, part):
    key_one, key_two = jax.random.split(jax.random.fold_in(key, 11), 2)

    def one_box(box_index):
        factor = jax.random.normal(jax.random.fold_in(key_one, box_index), (BOUND, BOUND), jnp.float32)
        crossed = jnp.dot(factor, factor.T, precision=lax.Precision.HIGHEST, preferred_element_type=jnp.float32)
        return (crossed + crossed.T) * (1.5 / BOUND)
    box_count = NBX * NBY
    wishart = lax.map(one_box, jnp.arange(box_count, dtype=jnp.int32)).reshape(NBX, NBY, BOUND, BOUND)
    diagonal = jnp.exp(jax.random.uniform(key_two, (NBX, NBY, BOUND), jnp.float32, jnp.log(0.25), jnp.log(2.0)))
    matrix = wishart + diagonal[:, :, :, None] * jnp.eye(BOUND, dtype=jnp.float32)
    return matrix


def levels(rng, shape, cuts, least, top_value):
    loudness, own = 1.0, jax.random.fold_in(rng, 6)
    for dim, parts in cuts:
        heights = jnp.exp(jax.random.uniform(jax.random.fold_in(own, dim), (parts,), jnp.float32, least / len(cuts), top_value / len(cuts)))
        loudness = loudness * jnp.repeat(heights, shape[dim] // parts).reshape([-1 if axis == dim else 1 for axis in range(len(shape))])
    return loudness


def normal_values(rng, shape, width, reach, shards=(), kind=jnp.bfloat16):
    drawn = jax.random.normal(rng, shape, jnp.float32) * width
    if len(shards) > 0:
        drawn = levels(rng, shape, shards, -0.22, 0.18) * drawn
    return jnp.clip(drawn, min=-reach, max=reach).astype(kind)


def setup_inputs(seed: int = 0) -> dict:
    seeds = jax.random.split(jax.random.key(seed), 4)
    dtn_maps = draw_dtn_maps(jax.random.fold_in(seeds[3], 71), 0)
    flux_part = normal_values(seeds[1], (NBX, NBY, BOUND, RHS), 1.0, 6.0, ((0, 8), (1, 4)), jnp.float32)
    outer_values = normal_values(seeds[2], (NBX, NBY, 2 * EDGE, RHS), 1.0, 6.0, ((0, 8), (1, 4)), jnp.float32)
    return dict(dtn_maps=dtn_maps, flux_part=flux_part, outer_values=outer_values)


west_keep = [0, 2, 3]
east_keep = [0, 1, 2]

def product(left, right):
    return jnp.dot(left.astype(jnp.float32), right.astype(jnp.float32), precision=lax.Precision.HIGHEST, preferred_element_type=jnp.float32)

def invert_spd(matrix):
    factor = jnp.linalg.cholesky(matrix)
    identity = jnp.eye(matrix.shape[0], dtype=jnp.float32)
    halfway = lax.linalg.triangular_solve(factor, identity, left_side=True, lower=True)
    return lax.linalg.triangular_solve(factor, halfway, left_side=True, lower=True, transpose_a=True)

def blocks(matrix, row_list, col_list):
    edge_len = matrix.shape[0] // 4
    shaped = matrix.reshape(4, edge_len, 4, edge_len)
    picked = shaped[jnp.array(row_list, dtype=jnp.int32)][:, :, jnp.array(col_list, dtype=jnp.int32)]
    return picked.reshape(len(row_list) * edge_len, len(col_list) * edge_len)

def take_sides(matrix, side_list, count):
    edge_len = matrix.shape[0] // count
    shaped = matrix.reshape(count, edge_len, matrix.shape[1])
    return shaped[jnp.array(side_list, dtype=jnp.int32)].reshape(len(side_list) * edge_len, matrix.shape[1])

def pick_cols(row_block, col_list):
    return row_block[:, jnp.array(col_list, dtype=jnp.int32)].reshape(row_block.shape[0], -1)

def merge_pair(west_map, east_map, west_flux, east_flux):
    edge_len = west_map.shape[0] // 4
    inner_sum = blocks(west_map, [1], [1]) + blocks(east_map, [3], [3])
    inverse = invert_spd(inner_sum)
    coupling = jnp.concatenate([blocks(west_map, [1], west_keep), blocks(east_map, [3], east_keep)], axis=1)
    solved = product(inverse, coupling)
    flux_sum = take_sides(west_flux, [1], 4) + take_sides(east_flux, [3], 4)
    solved_flux = product(inverse, flux_sum)
    blank_block = jnp.zeros((3 * edge_len, 3 * edge_len), jnp.float32)
    west_side = blocks(west_map, west_keep, [1])
    east_side = blocks(east_map, east_keep, [3])
    west_rows = jnp.concatenate([blocks(west_map, west_keep, west_keep), blank_block], axis=1) - product(west_side, solved)
    east_rows = jnp.concatenate([blank_block, blocks(east_map, east_keep, east_keep)], axis=1) - product(east_side, solved)
    west_out = take_sides(west_flux, west_keep, 4) - product(west_side, solved_flux)
    east_out = take_sides(east_flux, east_keep, 4) - product(east_side, solved_flux)
    return (west_rows, east_rows, west_out, east_out, solved, solved_flux)

def merge_group(maps, fluxes, outer):
    edge_len = maps.shape[2] // 4
    low_west, low_east, lflux_west, lflux_east, low_solve, low_fsolve = merge_pair(maps[0, 0], maps[1, 0], fluxes[0, 0], fluxes[1, 0])
    up_west, up_east, uflux_west, uflux_east, up_solve, up_fsolve = merge_pair(maps[0, 1], maps[1, 1], fluxes[0, 1], fluxes[1, 1])
    lower_box = jnp.concatenate([take_sides(low_west, [1], 3), take_sides(low_east, [2], 3)], axis=0).reshape(2 * edge_len, 6, edge_len)
    upper_box = jnp.concatenate([take_sides(up_west, [0], 3), take_sides(up_east, [0], 3)], axis=0).reshape(2 * edge_len, 6, edge_len)
    inner_sum = pick_cols(lower_box, [1, 5]) + pick_cols(upper_box, [0, 3])
    coupling = jnp.concatenate([pick_cols(lower_box, [0, 2, 3, 4]), pick_cols(upper_box, [1, 2, 4, 5])], axis=1)
    inverse = invert_spd(inner_sum)
    solved = product(inverse, coupling)
    flux_sum = jnp.concatenate([take_sides(lflux_west, [1], 3) + take_sides(uflux_west, [0], 3), take_sides(lflux_east, [2], 3) + take_sides(uflux_east, [0], 3)], axis=0)
    solved_flux = product(inverse, flux_sum)

    def final_rows(row_set, flux_set, kept_list, box_cols, inner_cols, upper_flag):
        row_part = take_sides(row_set, kept_list, 3).reshape(2 * edge_len, 6, edge_len)
        across = pick_cols(row_part, inner_cols)
        own_cols = pick_cols(row_part, box_cols)
        blank_block = jnp.zeros_like(own_cols)
        if upper_flag:
            placed = jnp.concatenate([blank_block, own_cols], axis=1)
        else:
            placed = jnp.concatenate([own_cols, blank_block], axis=1)
        return (placed - product(across, solved), take_sides(flux_set, kept_list, 3) - product(across, solved_flux))
    map00, flux00 = final_rows(low_west, lflux_west, [0, 2], [0, 2, 3, 4], [1, 5], False)
    map10, flux10 = final_rows(low_east, lflux_east, [0, 1], [0, 2, 3, 4], [1, 5], False)
    map01, flux01 = final_rows(up_west, uflux_west, [1, 2], [1, 2, 4, 5], [0, 3], True)
    map11, flux11 = final_rows(up_east, uflux_east, [1, 2], [1, 2, 4, 5], [0, 3], True)
    outer00, outer10, outer01, outer11 = (outer[0, 0], outer[1, 0], outer[0, 1], outer[1, 1])
    gathered = jnp.concatenate([outer00, outer10, outer01, outer11], axis=0)
    inner_values = -(product(solved, gathered) + solved_flux)
    west_half = inner_values[:edge_len]
    east_half = inner_values[edge_len:]
    lower_ext = jnp.concatenate([outer00[:edge_len], west_half, outer00[edge_len:], outer10[:edge_len], outer10[edge_len:], east_half], axis=0)
    upper_ext = jnp.concatenate([west_half, outer01[:edge_len], outer01[edge_len:], east_half, outer11[:edge_len], outer11[edge_len:]], axis=0)
    low_inner = -(product(low_solve, lower_ext) + low_fsolve)
    up_inner = -(product(up_solve, upper_ext) + up_fsolve)
    box00 = jnp.concatenate([outer00[:edge_len], low_inner, west_half, outer00[edge_len:]], axis=0)
    box10 = jnp.concatenate([outer10[:edge_len], outer10[edge_len:], east_half, low_inner], axis=0)
    box01 = jnp.concatenate([west_half, up_inner, outer01[:edge_len], outer01[edge_len:]], axis=0)
    box11 = jnp.concatenate([east_half, outer11[:edge_len], outer11[edge_len:], up_inner], axis=0)
    maps_out = jnp.stack([jnp.stack([map00, map01]), jnp.stack([map10, map11])])
    flux_out = jnp.stack([jnp.stack([flux00, flux01]), jnp.stack([flux10, flux11])])
    boxes_out = jnp.stack([jnp.stack([box00, box01]), jnp.stack([box10, box11])])
    return (maps_out, flux_out, boxes_out)

def grouped(array_in):
    return array_in.reshape(2, NBX // 2, 2, NBY // 2, array_in.shape[2], array_in.shape[3]).transpose(1, 3, 0, 2, 4, 5).reshape(-1, 2, 2, array_in.shape[2], array_in.shape[3])

def ungrouped(array_in):
    return array_in.reshape(NBX // 2, NBY // 2, 2, 2, array_in.shape[3], array_in.shape[4]).transpose(2, 0, 3, 1, 4, 5).reshape(NBX, NBY, array_in.shape[3], array_in.shape[4])

def reference(dtn_maps, flux_part, outer_values):
    results = lax.map(lambda group_items: merge_group(group_items[0], group_items[1], group_items[2]), (grouped(dtn_maps), grouped(flux_part), grouped(outer_values)))
    return (ungrouped(results[0]), ungrouped(results[1]), ungrouped(results[2]))
```

```python
import functools

import jax
import jax.numpy as jnp
from jax import lax
from jax.experimental import pallas as pl
from jax.experimental.pallas import tpu as pltpu
from jax.sharding import PartitionSpec as P

VMEM = pl.BlockSpec(memory_space=pltpu.VMEM)
SMEM = pl.BlockSpec(memory_space=pltpu.SMEM)
PARAMS = pltpu.CompilerParams(vmem_limit_bytes=60 * 2**20)

NN = (((1,), (0,)), ((), ()))
TN = (((0,), (0,)), ((), ()))
NT = (((1,), (1,)), ((), ()))


def split(value):
    high = value.astype(jnp.bfloat16)
    low = (value - high.astype(jnp.float32)).astype(jnp.bfloat16)
    return high, low


def dot_split(left, right, dims=NN):
    one = functools.partial(
        lax.dot_general, dimension_numbers=dims, preferred_element_type=jnp.float32
    )
    left_high, left_low = left
    right_high, right_low = right
    return one(left_high, right_high) + (one(left_high, right_low) + one(left_low, right_high))


def dot3(left, right, dims=NN):
    return dot_split(split(left), split(right), dims)


def dot6(left, right, dims=NN):
    return lax.dot_general(
        left,
        right,
        dims,
        precision=lax.Precision.HIGHEST,
        preferred_element_type=jnp.float32,
    )


def unit(size):
    rows = lax.broadcasted_iota(jnp.int32, (size, size), 0)
    cols = lax.broadcasted_iota(jnp.int32, (size, size), 1)
    return jnp.where(rows == cols, 1.0, 0.0).astype(jnp.float32)


def row_norm(value):
    return jnp.max(jnp.sum(jnp.abs(value), axis=1, keepdims=True))


def invert_spd(matrix_ref, out_ref, power_ref):
    size = matrix_ref.shape[0]
    matrix = matrix_ref[...]
    sums = jnp.max(jnp.sum(jnp.abs(matrix), axis=1, keepdims=True), axis=0, keepdims=True)
    scale = 1.0 / sums
    first = unit(size) - scale * matrix
    out_ref[...] = scale * (unit(size) + first)
    power_ref[...] = dot3(first, first)

    def more(state):
        count, norm = state
        return jnp.logical_and(norm > 1e-3, count < 40)

    def double(state):
        count, _ = state
        power = power_ref[...]
        parts = split(power)
        out = out_ref[...]
        out_ref[...] = out + dot_split(split(out), parts)
        square = dot_split(parts, parts)
        power_ref[...] = square
        return count + 1, row_norm(square)

    lax.while_loop(more, double, (jnp.int32(0), row_norm(power_ref[...])))

    def correct(state):
        count, _ = state
        rest = unit(size) - dot6(matrix_ref[...], out_ref[...])
        out = out_ref[...]
        out_ref[...] = out + dot3(out, rest)
        return count + 1, row_norm(rest)

    lax.while_loop(more, correct, (jnp.int32(0), jnp.float32(1.0)))


def pair_kernel(bit_ref, own_ref, other_ref, inv_ref, solve_ref, part_ref, sum_ref, power_ref, joint_ref):
    edge = own_ref.shape[0]
    bit = bit_ref[0]
    near = pl.ds(pl.multiple_of(bit * edge, edge), edge)
    far = pl.ds(pl.multiple_of((1 - bit) * edge, edge), edge)
    sum_ref[...] = own_ref[:, :edge] + other_ref[:, :edge]
    joint_ref[:, near] = own_ref[:, edge : 2 * edge]
    joint_ref[:, far] = other_ref[:, edge : 2 * edge]
    invert_spd(sum_ref, inv_ref, power_ref)
    joint = joint_ref[...]
    solve = dot6(inv_ref[...], joint)
    solve_ref[...] = solve
    part_ref[...] = -dot6(joint, solve, TN)
    part_ref[near, near] += own_ref[:, 2 * edge :]
    part_ref[far, far] += other_ref[:, 2 * edge :]


def pair_step(bit, own, other):
    edge = own.shape[0]
    shape = lambda *dims: jax.ShapeDtypeStruct(dims, jnp.float32)
    return pl.pallas_call(
        pair_kernel,
        out_shape=(shape(edge, edge), shape(edge, 2 * edge), shape(2 * edge, 2 * edge)),
        in_specs=[SMEM, VMEM, VMEM],
        out_specs=(VMEM, VMEM, VMEM),
        scratch_shapes=[
            pltpu.VMEM((edge, edge), jnp.float32),
            pltpu.VMEM((edge, edge), jnp.float32),
            pltpu.VMEM((edge, 2 * edge), jnp.float32),
        ],
        compiler_params=PARAMS,
        cost_estimate=pl.CostEstimate(
            flops=200 * edge**3, bytes_accessed=16 * edge * edge * 4, transcendentals=0
        ),
        name="pair_step",
    )(bit, own, other)


def block_kernel(own_ref, other_ref, inv_ref, lead_ref, lead_inv_ref, power_ref):
    edge = lead_ref.shape[0]
    lead_ref[...] = own_ref[:edge, :edge] + other_ref[:edge, :edge]
    invert_spd(lead_ref, lead_inv_ref, power_ref)
    lead_inv = lead_inv_ref[...]
    cross = own_ref[edge:, :edge] + other_ref[edge:, :edge]
    ratio = dot6(cross, lead_inv)
    lead_ref[...] = own_ref[edge:, edge:] + other_ref[edge:, edge:] - dot6(ratio, cross, NT)
    invert_spd(lead_ref, lead_inv_ref, power_ref)
    tail_inv = lead_inv_ref[...]
    lower = -dot6(tail_inv, ratio)
    inv_ref[edge:, edge:] = tail_inv
    inv_ref[edge:, :edge] = lower
    inv_ref[:edge, edge:] = lower.T
    inv_ref[:edge, :edge] = lead_inv - dot6(ratio, lower, TN)


def block_step(own, other):
    size = own.shape[0]
    edge = size // 2
    return pl.pallas_call(
        block_kernel,
        out_shape=jax.ShapeDtypeStruct((size, size), jnp.float32),
        in_specs=[VMEM, VMEM],
        out_specs=VMEM,
        scratch_shapes=[pltpu.VMEM((edge, edge), jnp.float32)] * 3,
        compiler_params=PARAMS,
        cost_estimate=pl.CostEstimate(
            flops=400 * edge**3, bytes_accessed=12 * edge * edge * 4, transcendentals=0
        ),
        name="block_step",
    )(own, other)


def across_kernel(bit_ref, solve_ref, sides_ref, out_ref):
    edge = solve_ref.shape[0]
    slot = pl.ds(pl.multiple_of(bit_ref[0] * edge, edge), edge)
    out_ref[...] = -dot3(solve_ref[...], sides_ref[:edge, :], TN)
    out_ref[slot, :] += sides_ref[edge:, :]


def across_step(bit, solve, sides):
    size = sides.shape[0]
    return pl.pallas_call(
        across_kernel,
        out_shape=jax.ShapeDtypeStruct((size, size), jnp.float32),
        in_specs=[SMEM, VMEM, VMEM],
        out_specs=VMEM,
        compiler_params=PARAMS,
        cost_estimate=pl.CostEstimate(
            flops=3 * size**3, bytes_accessed=10 * size * size, transcendentals=0
        ),
        name="across_step",
    )(bit, solve, sides)


def merge_kernel(
    bits_ref,
    inv_ref,
    binv_ref,
    solve_ref,
    solve_far_ref,
    kept_ref,
    sides_a_ref,
    sides_b_ref,
    across_a_ref,
    across_b_ref,
    across_c_ref,
    across_d_ref,
    data_a_ref,
    data_b_ref,
    data_c_ref,
    data_d_ref,
    map_ref,
    flux_ref,
    box_ref,
    inner_ref,
):
    edge = inv_ref.shape[0]
    two = 2 * edge
    bit_x, bit_y, side_e, side_i, side_0, side_1 = [bits_ref[index] for index in range(6)]

    def rows(slot, size):
        return pl.ds(pl.multiple_of(slot * size, size), size)

    near_x, far_x = rows(bit_x, edge), rows(1 - bit_x, edge)
    inv = inv_ref[...]
    data_a, data_b, data_c, data_d = (
        data_a_ref[...],
        data_b_ref[...],
        data_c_ref[...],
        data_d_ref[...],
    )
    binv_parts = split(binv_ref[...])
    across_a = split(across_a_ref[...])
    head = split(dot_split(across_a, binv_parts, TN))
    kept_a = sides_a_ref[:edge, :]
    kept_b = sides_b_ref[:edge, :]
    kept_a_parts = split(kept_a)
    kept_b_parts = split(kept_b)
    left = split(dot_split(kept_a_parts, split(inv), TN))

    def slot(flip_x, flip_y):
        along = 1 - bit_x if flip_x else bit_x
        up = 1 - bit_y if flip_y else bit_y
        return rows(along + 2 * up, two)

    across_b = split(across_b_ref[...])
    across_c = split(across_c_ref[...])
    across_d = split(across_d_ref[...])
    map_ref[:, slot(False, False)] = (
        kept_ref[...] - dot_split(left, kept_a_parts) - dot_split(head, across_a)
    )
    map_ref[:, slot(True, False)] = -dot_split(left, kept_b_parts) - dot_split(head, across_b)
    map_ref[:, slot(False, True)] = -dot_split(head, across_c)
    map_ref[:, slot(True, True)] = -dot_split(head, across_d)

    sum_near = data_a[:, :edge] + data_b[:, :edge]
    sum_far = data_c[:, :edge] + data_d[:, :edge]
    inner_ref[:, near_x] = data_a[:, edge:two] + data_c[:, edge:two]
    inner_ref[:, far_x] = data_b[:, edge:two] + data_d[:, edge:two]
    solve = split(solve_ref[...])
    near_parts = split(sum_near)
    block_sum = (
        inner_ref[...]
        - dot_split(near_parts, solve)
        - dot_split(split(sum_far), split(solve_far_ref[...]))
    )
    outer = [split(data[:, two : 2 * two]) for data in (data_a, data_b, data_c, data_d)]
    flux_ref[...] = (
        data_a[:, 2 * two :]
        - dot_split(near_parts, left, NT)
        - dot_split(split(block_sum), head, NT)
    ).T
    total = block_sum
    for values, across in zip(outer, (across_a, across_b, across_c, across_d)):
        total = total + dot_split(values, across, NT)
    inner = -dot_split(split(total), binv_parts)
    inner_ref[...] = inner
    pair_sum = (
        sum_near + dot_split(outer[0], kept_a_parts, NT) + dot_split(outer[1], kept_b_parts, NT)
    )
    pair_inner = -dot_split(split(pair_sum), split(inv)) - dot_split(split(inner), solve, NT)
    box_ref[rows(side_e, edge), :] = pair_inner.T
    box_ref[rows(side_i, edge), :] = inner_ref[:, near_x].T
    box_ref[rows(side_0, edge), :] = data_a[:, two : two + edge].T
    box_ref[rows(side_1, edge), :] = data_a[:, two + edge : 2 * two].T


def merge_step(*args):
    edge = args[1].shape[0]
    count = args[-1].shape[0]
    shape = lambda *dims: jax.ShapeDtypeStruct(dims, jnp.float32)
    return pl.pallas_call(
        merge_kernel,
        out_shape=(shape(2 * edge, 8 * edge), shape(2 * edge, count), shape(4 * edge, count)),
        in_specs=[SMEM] + [VMEM] * (len(args) - 1),
        out_specs=(VMEM, VMEM, VMEM),
        scratch_shapes=[pltpu.VMEM((count, 2 * edge), jnp.float32)],
        compiler_params=PARAMS,
        cost_estimate=pl.CostEstimate(
            flops=300 * edge**3, bytes_accessed=60 * edge * edge * 4, transcendentals=0
        ),
        name="merge_step",
    )(*args)


def partner(value, axis):
    count = lax.axis_size(axis)
    return lax.ppermute(value, axis, [(source, source ^ (count // 2)) for source in range(count)])


def on_device(dtn_maps, flux_part, outer_values):
    edge = dtn_maps.shape[2] // 4
    box_map, flux, outer = dtn_maps[0, 0], flux_part[0, 0], outer_values[0, 0]
    bit_x = (lax.axis_index("gx") // (lax.axis_size("gx") // 2)).astype(jnp.int32)
    bit_y = (lax.axis_index("gy") // (lax.axis_size("gy") // 2)).astype(jnp.int32)
    side_e = 1 + 2 * bit_x
    side_i = 2 - 2 * bit_y
    side_0 = bit_y * (2 - bit_x)
    side_1 = 3 - 2 * bit_x + bit_x * bit_y

    def block(row, col):
        return lax.dynamic_slice(box_map, (row * edge, col * edge), (edge, edge))

    def side(values, row):
        return lax.dynamic_slice_in_dim(values, row * edge, edge, 0)

    core = jnp.concatenate(
        [block(side_e, side_e), block(side_e, side_i), block(side_i, side_i)], axis=1
    )
    sides = jnp.concatenate(
        [
            jnp.concatenate([block(side_e, side_0), block(side_e, side_1)], axis=1),
            jnp.concatenate([block(side_i, side_0), block(side_i, side_1)], axis=1),
        ],
        axis=0,
    )
    kept = jnp.concatenate(
        [
            jnp.concatenate([block(side_0, side_0), block(side_0, side_1)], axis=1),
            jnp.concatenate([block(side_1, side_0), block(side_1, side_1)], axis=1),
        ],
        axis=0,
    )
    data = jnp.concatenate(
        [
            side(flux, side_e),
            side(flux, side_i),
            outer,
            side(flux, side_0),
            side(flux, side_1),
        ],
        axis=0,
    ).T
    shared = data[:, : 4 * edge]
    core_b = partner(core, "gx")
    core_c = partner(core, "gy")
    shared_b = partner(shared, "gx")
    sides_b = partner(sides, "gx")
    core_d = partner(core_b, "gy")
    sides_c = partner(sides, "gy")
    shared_c = partner(shared, "gy")
    shared_d = partner(shared_b, "gy")
    sides_d = partner(sides_b, "gy")

    near = bit_x[None]
    far = 1 - near
    inv, solve, part = pair_step(near, core, core_b)
    _, solve_far, part_far = pair_step(near, core_c, core_d)
    binv = block_step(part, part_far)
    across_a = across_step(near, solve, sides)
    across_c = across_step(near, solve_far, sides_c)
    across_b = across_step(far, solve, sides_b)
    across_d = across_step(far, solve_far, sides_d)
    bits = jnp.stack([bit_x, bit_y, side_e, side_i, side_0, side_1])
    merged_map, merged_flux, box_values = merge_step(
        bits,
        inv,
        binv,
        solve,
        solve_far,
        kept,
        sides,
        sides_b,
        across_a,
        across_b,
        across_c,
        across_d,
        data,
        shared_b,
        shared_c,
        shared_d,
    )
    return merged_map[None, None], merged_flux[None, None], box_values[None, None]


def solution(mesh):
    placed = P("gx", "gy", None, None)
    return jax.shard_map(
        on_device,
        mesh=mesh,
        in_specs=(placed, placed, placed),
        out_specs=(placed, placed, placed),
        check_vma=False,
    )
```

```python
import functools

import jax
import jax.numpy as jnp
from jax import lax
from jax.experimental import pallas as pl
from jax.experimental.pallas import tpu as pltpu
from jax.sharding import PartitionSpec as P

VMEM = pl.BlockSpec(memory_space=pltpu.VMEM)
SMEM = pl.BlockSpec(memory_space=pltpu.SMEM)
PARAMS = pltpu.CompilerParams(vmem_limit_bytes=60 * 2**20)

NN = (((1,), (0,)), ((), ()))
TN = (((0,), (0,)), ((), ()))
NT = (((1,), (1,)), ((), ()))


def split(value):
    high = value.astype(jnp.bfloat16)
    low = (value - high.astype(jnp.float32)).astype(jnp.bfloat16)
    return high, low


def dot_split(left, right, dims=NN):
    one = functools.partial(
        lax.dot_general, dimension_numbers=dims, preferred_element_type=jnp.float32
    )
    left_high, left_low = left
    right_high, right_low = right
    return one(left_high, right_high) + (one(left_high, right_low) + one(left_low, right_high))


def dot3(left, right, dims=NN):
    return dot_split(split(left), split(right), dims)


def dot6(left, right, dims=NN):
    return lax.dot_general(
        left,
        right,
        dims,
        precision=lax.Precision.HIGHEST,
        preferred_element_type=jnp.float32,
    )


def unit(size):
    rows = lax.broadcasted_iota(jnp.int32, (size, size), 0)
    cols = lax.broadcasted_iota(jnp.int32, (size, size), 1)
    return jnp.where(rows == cols, 1.0, 0.0).astype(jnp.float32)


def row_norm(value):
    return jnp.max(jnp.sum(jnp.abs(value), axis=1, keepdims=True))


def invert_spd(matrix_ref, out_ref, power_ref):
    size = matrix_ref.shape[0]
    matrix = matrix_ref[...]
    sums = jnp.max(jnp.sum(jnp.abs(matrix), axis=1, keepdims=True), axis=0, keepdims=True)
    scale = 1.0 / sums
    first = unit(size) - scale * matrix
    out_ref[...] = scale * (unit(size) + first)
    power_ref[...] = dot3(first, first)

    def more(state):
        count, norm = state
        return jnp.logical_and(norm > 1e-3, count < 40)

    def double(state):
        count, _ = state
        power = power_ref[...]
        parts = split(power)
        out = out_ref[...]
        out_ref[...] = out + dot_split(split(out), parts)
        square = dot_split(parts, parts)
        power_ref[...] = square
        return count + 1, row_norm(square)

    lax.while_loop(more, double, (jnp.int32(0), row_norm(power_ref[...])))

    def correct(state):
        count, _ = state
        rest = unit(size) - dot6(matrix_ref[...], out_ref[...])
        out = out_ref[...]
        out_ref[...] = out + dot3(out, rest)
        return count + 1, row_norm(rest)

    lax.while_loop(more, correct, (jnp.int32(0), jnp.float32(1.0)))


def unpack(core_ref, index):
    half = core_ref.shape[0]
    base = 3 * half * index
    lead = core_ref[:, base : base + half]
    cross = core_ref[:, base + half : base + 2 * half]
    tail = core_ref[:, base + 2 * half : base + 3 * half]
    return jnp.concatenate(
        [
            jnp.concatenate([lead, cross], axis=1),
            jnp.concatenate([cross.T, tail], axis=1),
        ],
        axis=0,
    )


def pair_kernel(bit_ref, own_ref, other_ref, inv_ref, solve_ref, part_ref, sum_ref, power_ref, joint_ref):
    half = own_ref.shape[0]
    edge = 2 * half
    bit = bit_ref[0]
    near = pl.ds(pl.multiple_of(bit * edge, edge), edge)
    far = pl.ds(pl.multiple_of((1 - bit) * edge, edge), edge)
    sum_ref[...] = unpack(own_ref, 0) + unpack(other_ref, 0)
    for place, ref in ((near, own_ref), (far, other_ref)):
        joint_ref[:half, place] = ref[:, 3 * edge : 4 * edge]
        joint_ref[half:, place] = ref[:, 4 * edge : 5 * edge]
    invert_spd(sum_ref, inv_ref, power_ref)
    joint = joint_ref[...]
    solve = dot6(inv_ref[...], joint)
    solve_ref[...] = solve
    part_ref[...] = -dot6(joint, solve, TN)
    part_ref[near, near] += unpack(own_ref, 1)
    part_ref[far, far] += unpack(other_ref, 1)


def pair_step(bit, own, other):
    edge = 2 * own.shape[0]
    shape = lambda *dims: jax.ShapeDtypeStruct(dims, jnp.float32)
    return pl.pallas_call(
        pair_kernel,
        out_shape=(shape(edge, edge), shape(edge, 2 * edge), shape(2 * edge, 2 * edge)),
        in_specs=[SMEM, VMEM, VMEM],
        out_specs=(VMEM, VMEM, VMEM),
        scratch_shapes=[
            pltpu.VMEM((edge, edge), jnp.float32),
            pltpu.VMEM((edge, edge), jnp.float32),
            pltpu.VMEM((edge, 2 * edge), jnp.float32),
        ],
        compiler_params=PARAMS,
        cost_estimate=pl.CostEstimate(
            flops=200 * edge**3, bytes_accessed=16 * edge * edge * 4, transcendentals=0
        ),
        name="pair_step",
    )(bit, own, other)


def block_kernel(
    bit_ref,
    own_ref,
    other_ref,
    pair_inv_ref,
    solve_ref,
    solve_far_ref,
    sides_ref,
    inv_ref,
    head_ref,
    left_ref,
    near_ref,
    far_ref,
    lead_ref,
    lead_inv_ref,
    power_ref,
    across_ref,
):
    edge = lead_ref.shape[0]
    lead_ref[...] = own_ref[:edge, :edge] + other_ref[:edge, :edge]
    invert_spd(lead_ref, lead_inv_ref, power_ref)
    lead_inv = lead_inv_ref[...]
    cross = own_ref[edge:, :edge] + other_ref[edge:, :edge]
    ratio = dot6(cross, lead_inv)
    lead_ref[...] = own_ref[edge:, edge:] + other_ref[edge:, edge:] - dot6(ratio, cross, NT)
    invert_spd(lead_ref, lead_inv_ref, power_ref)
    tail_inv = lead_inv_ref[...]
    lower = -dot6(tail_inv, ratio)
    inv_ref[edge:, edge:] = tail_inv
    inv_ref[edge:, :edge] = lower
    inv_ref[:edge, edge:] = lower.T
    inv_ref[:edge, :edge] = lead_inv - dot6(ratio, lower, TN)

    slot = pl.ds(pl.multiple_of(bit_ref[0] * edge, edge), edge)
    solve = split(solve_ref[...])
    kept = split(sides_ref[:edge, :])
    across_ref[...] = -dot_split(solve, kept, TN)
    across_ref[slot, :] += sides_ref[edge:, :]
    head = dot3(across_ref[...], inv_ref[...], TN)
    head_ref[...] = head
    head = split(head)
    left = dot_split(kept, split(pair_inv_ref[...]), TN)
    left_ref[...] = left
    near_ref[...] = left - dot_split(head, solve, NT)
    far_ref[...] = -dot_split(head, split(solve_far_ref[...]), NT)


def block_step(bit, own, *rest):
    size = own.shape[0]
    edge = size // 2
    shape = lambda *dims: jax.ShapeDtypeStruct(dims, jnp.float32)
    return pl.pallas_call(
        block_kernel,
        out_shape=(shape(size, size), shape(size, size)) + (shape(size, edge),) * 3,
        in_specs=[SMEM] + [VMEM] * 6,
        out_specs=(VMEM,) * 5,
        scratch_shapes=[pltpu.VMEM((edge, edge), jnp.float32)] * 3
        + [pltpu.VMEM((size, size), jnp.float32)],
        compiler_params=PARAMS,
        cost_estimate=pl.CostEstimate(
            flops=600 * edge**3, bytes_accessed=30 * edge * edge * 4, transcendentals=0
        ),
        name="block_step",
    )(bit, own, *rest)


def merge_kernel(
    bits_ref,
    inv_ref,
    binv_ref,
    head_ref,
    left_ref,
    near_ref,
    far_ref,
    solve_ref,
    solve_far_ref,
    kept_ref,
    sides_a_ref,
    sides_b0_ref,
    sides_b1_ref,
    sides_c_ref,
    sides_d0_ref,
    sides_d1_ref,
    data_a_ref,
    data_b_ref,
    data_c_ref,
    data_d_ref,
    map_ref,
    flux_ref,
    box_ref,
    inner_ref,
    work_ref,
    sems,
):
    edge = inv_ref.shape[0]
    two = 2 * edge
    bit_x, bit_y, side_e, side_i, side_0, side_1 = [bits_ref[index] for index in range(6)]

    def rows(slot, size):
        return pl.ds(pl.multiple_of(slot * size, size), size)

    near_x, far_x = rows(bit_x, edge), rows(1 - bit_x, edge)
    near = split(near_ref[...])
    far = split(far_ref[...])
    head_near = split(head_ref[:, near_x])
    head_far = split(head_ref[:, far_x])
    copies = []

    def put(index, along, up, lead, tail, pieces, base=None):
        for count, (top, low) in enumerate(pieces):
            part = slice(index * two + count * edge, index * two + (count + 1) * edge)
            value = -dot_split(lead, top) - dot_split(tail, low)
            if base is not None:
                value = value + base[:, count * edge : (count + 1) * edge]
            work_ref[:, part] = value
        copy = pltpu.make_async_copy(
            work_ref.at[:, pl.ds(index * two, two)],
            map_ref.at[:, rows(along + 2 * up, two)],
            sems.at[index],
        )
        copy.start()
        copies.append(copy)

    def whole(ref):
        return [
            (split(ref[:edge, :edge]), split(ref[edge:, :edge])),
            (split(ref[:edge, edge:]), split(ref[edge:, edge:])),
        ]

    def halves(*refs):
        return [(split(ref[:edge, :]), split(ref[edge:, :])) for ref in refs]

    side_a = whole(sides_a_ref)
    side_b = halves(sides_b0_ref, sides_b1_ref)
    side_c = whole(sides_c_ref)
    side_d = halves(sides_d0_ref, sides_d1_ref)
    put(0, bit_x, bit_y, near, head_near, side_a, kept_ref[...])
    put(1, 1 - bit_x, bit_y, near, head_far, side_b)
    put(2, bit_x, 1 - bit_y, far, head_near, side_c)
    put(3, 1 - bit_x, 1 - bit_y, far, head_far, side_d)

    refs = (data_a_ref, data_b_ref, data_c_ref, data_d_ref)
    sum_near = data_a_ref[:, :edge] + data_b_ref[:, :edge]
    sum_far = data_c_ref[:, :edge] + data_d_ref[:, :edge]
    top = []
    low = []
    for ref, side in zip(refs, (side_a, side_b, side_c, side_d)):
        values = [split(ref[:, two + count * edge : two + (count + 1) * edge]) for count in (0, 1)]
        top.append(sum(dot_split(value, piece[0], NT) for value, piece in zip(values, side)))
        low.append(sum(dot_split(value, piece[1], NT) for value, piece in zip(values, side)))
    inv = split(inv_ref[...])
    solve = split(solve_ref[...])
    solve_far = split(solve_far_ref[...])
    inner_ref[:, near_x] = data_a_ref[:, edge:two] + data_c_ref[:, edge:two]
    inner_ref[:, far_x] = data_b_ref[:, edge:two] + data_d_ref[:, edge:two]
    near_sum = split(sum_near)
    block_sum = (
        inner_ref[...] - dot_split(near_sum, solve) - dot_split(split(sum_far), solve_far)
    )
    flux_ref[...] = (
        data_a_ref[:, 2 * two :]
        - dot_split(near_sum, split(left_ref[...]), NT)
        - dot_split(split(block_sum), split(head_ref[...]), NT)
    )
    pair_near = top[0] + top[1]
    inner_ref[:, near_x] = low[0] + low[2]
    inner_ref[:, far_x] = low[1] + low[3]
    total = (
        block_sum
        + inner_ref[...]
        - dot_split(split(pair_near), solve)
        - dot_split(split(top[2] + top[3]), solve_far)
    )
    inner = -dot_split(split(total), split(binv_ref[...]))
    inner_ref[...] = inner
    pair_inner = -dot_split(split(sum_near + pair_near), inv) - dot_split(split(inner), solve, NT)
    box_ref[:, rows(side_e, edge)] = pair_inner
    box_ref[:, rows(side_i, edge)] = inner_ref[:, near_x]
    box_ref[:, rows(side_0, edge)] = data_a_ref[:, two : two + edge]
    box_ref[:, rows(side_1, edge)] = data_a_ref[:, two + edge : 2 * two]
    for copy in copies:
        copy.wait()


def merge_step(*args):
    edge = args[1].shape[0]
    count = args[-1].shape[0]
    shape = lambda *dims: jax.ShapeDtypeStruct(dims, jnp.float32)
    return pl.pallas_call(
        merge_kernel,
        out_shape=(shape(2 * edge, 8 * edge), shape(count, 2 * edge), shape(count, 4 * edge)),
        in_specs=[SMEM] + [VMEM] * (len(args) - 1),
        out_specs=(pl.BlockSpec(memory_space=pl.ANY), VMEM, VMEM),
        scratch_shapes=[
            pltpu.VMEM((count, 2 * edge), jnp.float32),
            pltpu.VMEM((2 * edge, 8 * edge), jnp.float32),
            pltpu.SemaphoreType.DMA((4,)),
        ],
        compiler_params=PARAMS,
        cost_estimate=pl.CostEstimate(
            flops=300 * edge**3, bytes_accessed=60 * edge * edge * 4, transcendentals=0
        ),
        name="merge_step",
    )(*args)


def partner(value, axis):
    count = lax.axis_size(axis)
    return lax.ppermute(value, axis, [(source, source ^ (count // 2)) for source in range(count)])


def on_device(dtn_maps, flux_part, outer_values):
    edge = dtn_maps.shape[2] // 4
    box_map, flux, outer = dtn_maps[0, 0], flux_part[0, 0], outer_values[0, 0]
    bit_x = (lax.axis_index("gx") // (lax.axis_size("gx") // 2)).astype(jnp.int32)
    bit_y = (lax.axis_index("gy") // (lax.axis_size("gy") // 2)).astype(jnp.int32)
    side_e = 1 + 2 * bit_x
    side_i = 2 - 2 * bit_y
    side_0 = bit_y * (2 - bit_x)
    side_1 = 3 - 2 * bit_x + bit_x * bit_y

    def block(row, col):
        return lax.dynamic_slice(box_map, (row * edge, col * edge), (edge, edge))

    def side(values, row):
        return lax.dynamic_slice_in_dim(values, row * edge, edge, 0)

    half = edge // 2

    def halves(row, col, across, down):
        start = (row * edge + across * half, col * edge + down * half)
        return lax.dynamic_slice(box_map, start, (half, half))

    def packed(row):
        return [halves(row, row, 0, 0), halves(row, row, 0, 1), halves(row, row, 1, 1)]

    def strip(number):
        start = (side_e * edge + number * half, side_i * edge)
        return lax.dynamic_slice(box_map, start, (half, edge))

    core = jnp.concatenate(packed(side_e) + packed(side_i) + [strip(0), strip(1)], axis=1)
    sides_0 = jnp.concatenate([block(side_e, side_0), block(side_i, side_0)], axis=0)
    sides_1 = jnp.concatenate([block(side_e, side_1), block(side_i, side_1)], axis=0)
    sides = jnp.concatenate([sides_0, sides_1], axis=1)
    kept = jnp.concatenate(
        [
            jnp.concatenate([block(side_0, side_0), block(side_0, side_1)], axis=1),
            jnp.concatenate([block(side_1, side_0), block(side_1, side_1)], axis=1),
        ],
        axis=0,
    )
    data = jnp.concatenate(
        [
            side(flux, side_e),
            side(flux, side_i),
            outer,
            side(flux, side_0),
            side(flux, side_1),
        ],
        axis=0,
    ).T
    shared = data[:, : 4 * edge]
    core_b = partner(core, "gx")
    core_c = partner(core, "gy")
    sides_c = partner(sides, "gy")
    shared_c = partner(shared, "gy")
    sides_0, core_b, core_c, sides_c, shared_c = lax.optimization_barrier(
        (sides_0, core_b, core_c, sides_c, shared_c)
    )
    core_d = partner(core_b, "gy")
    sides_b0 = partner(sides_0, "gx")
    shared_b = partner(shared, "gx")

    near = bit_x[None]
    inv, solve, part = pair_step(near, core, core_b)
    _, solve_far, part_far = pair_step(near, core_c, core_d)
    sides_1, sides_b0, part, part_far, shared_b = lax.optimization_barrier(
        (sides_1, sides_b0, part, part_far, shared_b)
    )
    sides_b1 = partner(sides_1, "gx")
    shared_d = partner(shared_b, "gy")
    sides_d0 = partner(sides_b0, "gy")
    sides_d1 = partner(sides_b1, "gy")

    binv, head, left, lead_near, lead_far = block_step(
        near, part, part_far, inv, solve, solve_far, sides
    )
    bits = jnp.stack([bit_x, bit_y, side_e, side_i, side_0, side_1])
    merged_map, merged_flux, box_values = merge_step(
        bits,
        inv,
        binv,
        head,
        left,
        lead_near,
        lead_far,
        solve,
        solve_far,
        kept,
        sides,
        sides_b0,
        sides_b1,
        sides_c,
        sides_d0,
        sides_d1,
        data,
        shared_b,
        shared_c,
        shared_d,
    )
    merged_flux, box_values = merged_flux.T, box_values.T
    return merged_map[None, None], merged_flux[None, None], box_values[None, None]


def solution(mesh):
    placed = P("gx", "gy", None, None)
    return jax.shard_map(
        on_device,
        mesh=mesh,
        in_specs=(placed, placed, placed),
        out_specs=(placed, placed, placed),
        check_vma=False,
    )
```

```python
import functools

import jax
import jax.numpy as jnp
from jax import lax
from jax.experimental import pallas as pl
from jax.experimental.pallas import tpu as pltpu
from jax.sharding import PartitionSpec as P

VMEM = pl.BlockSpec(memory_space=pltpu.VMEM)
SMEM = pl.BlockSpec(memory_space=pltpu.SMEM)
PARAMS = pltpu.CompilerParams(vmem_limit_bytes=60 * 2**20)

NN = (((1,), (0,)), ((), ()))
TN = (((0,), (0,)), ((), ()))
NT = (((1,), (1,)), ((), ()))


def split(value):
    high = value.astype(jnp.bfloat16)
    low = (value - high.astype(jnp.float32)).astype(jnp.bfloat16)
    return high, low


def dot_split(left, right, dims=NN):
    one = functools.partial(
        lax.dot_general, dimension_numbers=dims, preferred_element_type=jnp.float32
    )
    left_high, left_low = left
    right_high, right_low = right
    return one(left_high, right_high) + (one(left_high, right_low) + one(left_low, right_high))


def dot3(left, right, dims=NN):
    return dot_split(split(left), split(right), dims)


def dot6(left, right, dims=NN):
    return lax.dot_general(
        left,
        right,
        dims,
        precision=lax.Precision.HIGHEST,
        preferred_element_type=jnp.float32,
    )


def unit(size):
    rows = lax.broadcasted_iota(jnp.int32, (size, size), 0)
    cols = lax.broadcasted_iota(jnp.int32, (size, size), 1)
    return jnp.where(rows == cols, 1.0, 0.0).astype(jnp.float32)


def row_norm(value):
    return jnp.max(jnp.sum(jnp.abs(value), axis=1, keepdims=True))


def invert_spd(matrix_ref, out_ref, power_ref):
    size = matrix_ref.shape[0]
    matrix = matrix_ref[...]
    sums = jnp.max(jnp.sum(jnp.abs(matrix), axis=1, keepdims=True), axis=0, keepdims=True)
    scale = 1.0 / sums
    first = unit(size) - scale * matrix
    out_ref[...] = scale * (unit(size) + first)
    power_ref[...] = dot3(first, first)

    def more(state):
        count, norm = state
        return jnp.logical_and(norm > 1e-3, count < 40)

    def double(state):
        count, _ = state
        power = power_ref[...]
        parts = split(power)
        out = out_ref[...]
        out_ref[...] = out + dot_split(split(out), parts)
        square = dot_split(parts, parts)
        power_ref[...] = square
        return count + 1, row_norm(square)

    lax.while_loop(more, double, (jnp.int32(0), row_norm(power_ref[...])))

    def correct(state):
        count, _ = state
        rest = unit(size) - dot6(matrix_ref[...], out_ref[...])
        out = out_ref[...]
        out_ref[...] = out + dot3(out, rest)
        return count + 1, row_norm(rest)

    lax.while_loop(more, correct, (jnp.int32(0), jnp.float32(1.0)))


def unpack(core_ref, index):
    half = core_ref.shape[0]
    base = 3 * half * index
    lead = core_ref[:, base : base + half]
    cross = core_ref[:, base + half : base + 2 * half]
    tail = core_ref[:, base + 2 * half : base + 3 * half]
    return jnp.concatenate(
        [
            jnp.concatenate([lead, cross], axis=1),
            jnp.concatenate([cross.T, tail], axis=1),
        ],
        axis=0,
    )


def pack_kernel(sides_ref, map_ref, core_ref, sems):
    half = core_ref.shape[0]
    edge = 2 * half
    first, second = [pl.multiple_of(sides_ref[index] * edge, edge) for index in (0, 1)]
    pieces = [
        (first, first, 0, edge),
        (first + half, first + half, edge, half),
        (second, second, 3 * half, edge),
        (second + half, second + half, 3 * half + edge, half),
        (first, second, 3 * edge, edge),
        (first + half, second, 4 * edge, edge),
    ]
    copies = []
    for index, (row, col, place, width) in enumerate(pieces):
        row, col = pl.multiple_of(row, half), pl.multiple_of(col, half)
        copy = pltpu.make_async_copy(
            map_ref.at[pl.ds(row, half), pl.ds(col, width)],
            core_ref.at[:, pl.ds(place, width)],
            sems.at[index],
        )
        copy.start()
        copies.append(copy)
    for copy in copies:
        copy.wait()


def pack_step(sides, box_map):
    edge = box_map.shape[0] // 4
    return pl.pallas_call(
        pack_kernel,
        out_shape=jax.ShapeDtypeStruct((edge // 2, 5 * edge), jnp.float32),
        in_specs=[SMEM, pl.BlockSpec(memory_space=pl.ANY)],
        out_specs=VMEM,
        scratch_shapes=[pltpu.SemaphoreType.DMA((6,))],
        compiler_params=PARAMS,
        cost_estimate=pl.CostEstimate(flops=0, bytes_accessed=20 * edge * edge, transcendentals=0),
        name="pack_step",
    )(sides, box_map)


def pair_kernel(bit_ref, own_ref, other_ref, inv_ref, solve_ref, part_ref, sum_ref, power_ref, joint_ref):
    half = own_ref.shape[0]
    edge = 2 * half
    bit = bit_ref[0]
    near = pl.ds(pl.multiple_of(bit * edge, edge), edge)
    far = pl.ds(pl.multiple_of((1 - bit) * edge, edge), edge)
    sum_ref[...] = unpack(own_ref, 0) + unpack(other_ref, 0)
    for place, ref in ((near, own_ref), (far, other_ref)):
        joint_ref[:half, place] = ref[:, 3 * edge : 4 * edge]
        joint_ref[half:, place] = ref[:, 4 * edge : 5 * edge]
    invert_spd(sum_ref, inv_ref, power_ref)
    joint = joint_ref[...]
    solve = dot6(inv_ref[...], joint)
    solve_ref[...] = solve
    part_ref[...] = -dot6(joint, solve, TN)
    part_ref[near, near] += unpack(own_ref, 1)
    part_ref[far, far] += unpack(other_ref, 1)


def pair_step(bit, own, other):
    edge = 2 * own.shape[0]
    shape = lambda *dims: jax.ShapeDtypeStruct(dims, jnp.float32)
    return pl.pallas_call(
        pair_kernel,
        out_shape=(shape(edge, edge), shape(edge, 2 * edge), shape(2 * edge, 2 * edge)),
        in_specs=[SMEM, VMEM, VMEM],
        out_specs=(VMEM, VMEM, VMEM),
        scratch_shapes=[
            pltpu.VMEM((edge, edge), jnp.float32),
            pltpu.VMEM((edge, edge), jnp.float32),
            pltpu.VMEM((edge, 2 * edge), jnp.float32),
        ],
        compiler_params=PARAMS,
        cost_estimate=pl.CostEstimate(
            flops=200 * edge**3, bytes_accessed=16 * edge * edge * 4, transcendentals=0
        ),
        name="pair_step",
    )(bit, own, other)


def block_kernel(
    bit_ref,
    own_ref,
    other_ref,
    pair_inv_ref,
    solve_ref,
    solve_far_ref,
    sides_ref,
    inv_ref,
    head_ref,
    left_ref,
    near_ref,
    far_ref,
    lead_ref,
    lead_inv_ref,
    power_ref,
    across_ref,
):
    edge = lead_ref.shape[0]
    lead_ref[...] = own_ref[:edge, :edge] + other_ref[:edge, :edge]
    invert_spd(lead_ref, lead_inv_ref, power_ref)
    lead_inv = lead_inv_ref[...]
    cross = own_ref[edge:, :edge] + other_ref[edge:, :edge]
    ratio = dot6(cross, lead_inv)
    lead_ref[...] = own_ref[edge:, edge:] + other_ref[edge:, edge:] - dot6(ratio, cross, NT)
    invert_spd(lead_ref, lead_inv_ref, power_ref)
    tail_inv = lead_inv_ref[...]
    lower = -dot6(tail_inv, ratio)
    inv_ref[edge:, edge:] = tail_inv
    inv_ref[edge:, :edge] = lower
    inv_ref[:edge, edge:] = lower.T
    inv_ref[:edge, :edge] = lead_inv - dot6(ratio, lower, TN)

    slot = pl.ds(pl.multiple_of(bit_ref[0] * edge, edge), edge)
    solve = split(solve_ref[...])
    kept = split(sides_ref[:edge, :])
    across_ref[...] = -dot_split(solve, kept, TN)
    across_ref[slot, :] += sides_ref[edge:, :]
    head = dot3(across_ref[...], inv_ref[...], TN)
    head_ref[...] = head
    head = split(head)
    left = dot_split(kept, split(pair_inv_ref[...]), TN)
    left_ref[...] = left
    near_ref[...] = left - dot_split(head, solve, NT)
    far_ref[...] = -dot_split(head, split(solve_far_ref[...]), NT)


def block_step(bit, own, *rest):
    size = own.shape[0]
    edge = size // 2
    shape = lambda *dims: jax.ShapeDtypeStruct(dims, jnp.float32)
    return pl.pallas_call(
        block_kernel,
        out_shape=(shape(size, size), shape(size, size)) + (shape(size, edge),) * 3,
        in_specs=[SMEM] + [VMEM] * 6,
        out_specs=(VMEM,) * 5,
        scratch_shapes=[pltpu.VMEM((edge, edge), jnp.float32)] * 3
        + [pltpu.VMEM((size, size), jnp.float32)],
        compiler_params=PARAMS,
        cost_estimate=pl.CostEstimate(
            flops=600 * edge**3, bytes_accessed=30 * edge * edge * 4, transcendentals=0
        ),
        name="block_step",
    )(bit, own, *rest)


def merge_kernel(
    bits_ref,
    inv_ref,
    binv_ref,
    head_ref,
    left_ref,
    near_ref,
    far_ref,
    solve_ref,
    solve_far_ref,
    kept_ref,
    sides_a_ref,
    sides_b0_ref,
    sides_b1_ref,
    sides_c_ref,
    sides_d0_ref,
    sides_d1_ref,
    data_a_ref,
    data_b_ref,
    data_c_ref,
    data_d_ref,
    map_ref,
    flux_ref,
    box_ref,
    inner_ref,
    work_ref,
    sems,
):
    edge = inv_ref.shape[0]
    two = 2 * edge
    bit_x, bit_y, side_e, side_i, side_0, side_1 = [bits_ref[index] for index in range(6)]

    def rows(slot, size):
        return pl.ds(pl.multiple_of(slot * size, size), size)

    near_x, far_x = rows(bit_x, edge), rows(1 - bit_x, edge)
    near = split(near_ref[...])
    far = split(far_ref[...])
    head_near = split(head_ref[:, near_x])
    head_far = split(head_ref[:, far_x])
    copies = []

    def put(index, along, up, lead, tail, pieces, base=None):
        for count, (top, low) in enumerate(pieces):
            part = slice(index * two + count * edge, index * two + (count + 1) * edge)
            value = -dot_split(lead, top) - dot_split(tail, low)
            if base is not None:
                value = value + base[:, count * edge : (count + 1) * edge]
            work_ref[:, part] = value
        copy = pltpu.make_async_copy(
            work_ref.at[:, pl.ds(index * two, two)],
            map_ref.at[:, rows(along + 2 * up, two)],
            sems.at[index],
        )
        copy.start()
        copies.append(copy)

    def whole(ref):
        return [
            (split(ref[:edge, :edge]), split(ref[edge:, :edge])),
            (split(ref[:edge, edge:]), split(ref[edge:, edge:])),
        ]

    def halves(*refs):
        return [(split(ref[:edge, :]), split(ref[edge:, :])) for ref in refs]

    side_a = whole(sides_a_ref)
    side_b = halves(sides_b0_ref, sides_b1_ref)
    side_c = whole(sides_c_ref)
    side_d = halves(sides_d0_ref, sides_d1_ref)
    put(0, bit_x, bit_y, near, head_near, side_a, kept_ref[...])
    put(1, 1 - bit_x, bit_y, near, head_far, side_b)
    put(2, bit_x, 1 - bit_y, far, head_near, side_c)
    put(3, 1 - bit_x, 1 - bit_y, far, head_far, side_d)

    refs = (data_a_ref, data_b_ref, data_c_ref, data_d_ref)
    sum_near = data_a_ref[:, :edge] + data_b_ref[:, :edge]
    sum_far = data_c_ref[:, :edge] + data_d_ref[:, :edge]
    top = []
    low = []
    for ref, side in zip(refs, (side_a, side_b, side_c, side_d)):
        values = [split(ref[:, two + count * edge : two + (count + 1) * edge]) for count in (0, 1)]
        top.append(sum(dot_split(value, piece[0], NT) for value, piece in zip(values, side)))
        low.append(sum(dot_split(value, piece[1], NT) for value, piece in zip(values, side)))
    inv = split(inv_ref[...])
    solve = split(solve_ref[...])
    solve_far = split(solve_far_ref[...])
    inner_ref[:, near_x] = data_a_ref[:, edge:two] + data_c_ref[:, edge:two]
    inner_ref[:, far_x] = data_b_ref[:, edge:two] + data_d_ref[:, edge:two]
    near_sum = split(sum_near)
    block_sum = (
        inner_ref[...] - dot_split(near_sum, solve) - dot_split(split(sum_far), solve_far)
    )
    flux_ref[...] = (
        data_a_ref[:, 2 * two :]
        - dot_split(near_sum, split(left_ref[...]), NT)
        - dot_split(split(block_sum), split(head_ref[...]), NT)
    )
    pair_near = top[0] + top[1]
    inner_ref[:, near_x] = low[0] + low[2]
    inner_ref[:, far_x] = low[1] + low[3]
    total = (
        block_sum
        + inner_ref[...]
        - dot_split(split(pair_near), solve)
        - dot_split(split(top[2] + top[3]), solve_far)
    )
    inner = -dot_split(split(total), split(binv_ref[...]))
    inner_ref[...] = inner
    pair_inner = -dot_split(split(sum_near + pair_near), inv) - dot_split(split(inner), solve, NT)
    box_ref[:, rows(side_e, edge)] = pair_inner
    box_ref[:, rows(side_i, edge)] = inner_ref[:, near_x]
    box_ref[:, rows(side_0, edge)] = data_a_ref[:, two : two + edge]
    box_ref[:, rows(side_1, edge)] = data_a_ref[:, two + edge : 2 * two]
    for copy in copies:
        copy.wait()


def merge_step(*args):
    edge = args[1].shape[0]
    count = args[-1].shape[0]
    shape = lambda *dims: jax.ShapeDtypeStruct(dims, jnp.float32)
    return pl.pallas_call(
        merge_kernel,
        out_shape=(shape(2 * edge, 8 * edge), shape(count, 2 * edge), shape(count, 4 * edge)),
        in_specs=[SMEM] + [VMEM] * (len(args) - 1),
        out_specs=(pl.BlockSpec(memory_space=pl.ANY), VMEM, VMEM),
        scratch_shapes=[
            pltpu.VMEM((count, 2 * edge), jnp.float32),
            pltpu.VMEM((2 * edge, 8 * edge), jnp.float32),
            pltpu.SemaphoreType.DMA((4,)),
        ],
        compiler_params=PARAMS,
        cost_estimate=pl.CostEstimate(
            flops=300 * edge**3, bytes_accessed=60 * edge * edge * 4, transcendentals=0
        ),
        name="merge_step",
    )(*args)


def partner(value, axis):
    count = lax.axis_size(axis)
    return lax.ppermute(value, axis, [(source, source ^ (count // 2)) for source in range(count)])


def on_device(dtn_maps, flux_part, outer_values):
    edge = dtn_maps.shape[2] // 4
    box_map, flux, outer = dtn_maps[0, 0], flux_part[0, 0], outer_values[0, 0]
    bit_x = (lax.axis_index("gx") // (lax.axis_size("gx") // 2)).astype(jnp.int32)
    bit_y = (lax.axis_index("gy") // (lax.axis_size("gy") // 2)).astype(jnp.int32)
    side_e = 1 + 2 * bit_x
    side_i = 2 - 2 * bit_y
    side_0 = bit_y * (2 - bit_x)
    side_1 = 3 - 2 * bit_x + bit_x * bit_y

    def block(row, col):
        return lax.dynamic_slice(box_map, (row * edge, col * edge), (edge, edge))

    def side(values, row):
        return lax.dynamic_slice_in_dim(values, row * edge, edge, 0)

    core = pack_step(jnp.stack([side_e, side_i]), box_map)
    core, box_map = lax.optimization_barrier((core, box_map))
    sides_0 = jnp.concatenate([block(side_e, side_0), block(side_i, side_0)], axis=0)
    sides_1 = jnp.concatenate([block(side_e, side_1), block(side_i, side_1)], axis=0)
    sides = jnp.concatenate([sides_0, sides_1], axis=1)
    kept = jnp.concatenate(
        [
            jnp.concatenate([block(side_0, side_0), block(side_0, side_1)], axis=1),
            jnp.concatenate([block(side_1, side_0), block(side_1, side_1)], axis=1),
        ],
        axis=0,
    )
    data = jnp.concatenate(
        [
            side(flux, side_e),
            side(flux, side_i),
            outer,
            side(flux, side_0),
            side(flux, side_1),
        ],
        axis=0,
    ).T
    shared = data[:, : 4 * edge]
    core_b = partner(core, "gx")
    core_c = partner(core, "gy")
    sides_c = partner(sides, "gy")
    shared_c = partner(shared, "gy")
    sides_0, core_b, core_c, sides_c, shared_c = lax.optimization_barrier(
        (sides_0, core_b, core_c, sides_c, shared_c)
    )
    core_d = partner(core_b, "gy")
    sides_b0 = partner(sides_0, "gx")
    shared_b = partner(shared, "gx")

    near = bit_x[None]
    inv, solve, part = pair_step(near, core, core_b)
    _, solve_far, part_far = pair_step(near, core_c, core_d)
    sides_1, sides_b0, part, part_far, shared_b = lax.optimization_barrier(
        (sides_1, sides_b0, part, part_far, shared_b)
    )
    sides_b1 = partner(sides_1, "gx")
    shared_d = partner(shared_b, "gy")
    sides_d0 = partner(sides_b0, "gy")
    binv, head, left, lead_near, lead_far = block_step(
        near, part, part_far, inv, solve, solve_far, sides
    )
    sides_b1, binv = lax.optimization_barrier((sides_b1, binv))
    sides_d1 = partner(sides_b1, "gy")
    bits = jnp.stack([bit_x, bit_y, side_e, side_i, side_0, side_1])
    merged_map, merged_flux, box_values = merge_step(
        bits,
        inv,
        binv,
        head,
        left,
        lead_near,
        lead_far,
        solve,
        solve_far,
        kept,
        sides,
        sides_b0,
        sides_b1,
        sides_c,
        sides_d0,
        sides_d1,
        data,
        shared_b,
        shared_c,
        shared_d,
    )
    merged_flux, box_values = merged_flux.T, box_values.T
    return merged_map[None, None], merged_flux[None, None], box_values[None, None]


def solution(mesh):
    placed = P("gx", "gy", None, None)
    return jax.shard_map(
        on_device,
        mesh=mesh,
        in_specs=(placed, placed, placed),
        out_specs=(placed, placed, placed),
        check_vma=False,
    )
```
